32 devices in a mesh: blocks: 8 (over z, x), gz: 4 (over y, core).
Axes of the slice: x: 2, y: 2, z: 4, core: 2. Of those that a mesh axis runs over, the one named last changes fastest.
Arguments:
- coarse_field: float32 [4, 128, 3, 4096], P('gz', 'blocks'), may hold values from -6 to 6
- coarse_velocity: float32 [4, 128, 3, 4096], P('gz', 'blocks'), may hold values from -15 to 15
- fine_field: float32 [4, 96, 3, 4096], P('gz', 'blocks'), may hold values from -6 to 6
- fine_velocity: float32 [4, 96, 3, 4096], P('gz', 'blocks'), may hold values from -15 to 15
- pairs: int32 [4, 32, 6], P('gz', 'blocks'), may hold values from 0 to 15, as said below
Outputs:
- coarse_new: float32 [4, 128, 3, 4096], P('gz', 'blocks')
- fine_new: float32 [4, 96, 3, 4096], P('gz', 'blocks')
- face_jump: float32 [4, 32, 256], P('gz', 'blocks')
The draws below stay inside these ranges and needn't reach their ends.
Inputs may be any that keep to these rules, and one draw needn't show every extreme that they name: `pairs`: Columns: fine slot below 12, face axis 0 to 2, owner device below 8, coarse slot below 16, quadrant row and column 0 or 1. No two rows of a device name the same fine slot and face axis, and no two rows of a group name the same coarse block, face axis and quadrant. The rows of one device name one owner device at most 2 times, and exactly 2 times for some owner; rows of one device that name the same owner differ in face axis; some owner is named 2 times by every device of its group. Each face axis stands in 1 to 2 of a device's rows.
All inputs are finite; a program needn't handle non-finite values.
Results may differ from the reference program's by a relative error of at most 0.0003.
Values sent between devices are 32-bit elements; how exact they have to be, the bound alone decides.
A program may use at most 256 MiB of HBM per device.

```python
import jax
import jax.numpy as jnp
from jax import lax

EDGE = 16
HALF = 8
CB = 16
FB = 12
PAIRS_DEV = 4
COARSE_ALL = 128
FINE_ALL = 96
N_BLOCKS = 8
N_GZ = 4


def velocity_law(key, count):
    shape = (N_GZ, count * N_BLOCKS, 3, EDGE ** 3)
    group = jnp.arange(N_GZ)[:, None]
    device = jnp.arange(count * N_BLOCKS)[None, :] // count
    position = (device * N_GZ + group).astype(jnp.float32)
    scale = 1.0 + 2.0 * position / max(N_BLOCKS * N_GZ - 1, 1)
    first = jax.random.fold_in(key, 0)
    base = jax.random.truncated_normal(first, -5.0, 5.0, shape, jnp.float32)
    return (base * scale[:, :, None, None]).astype(jnp.float32)


def draw_coarse_velocity(key, part):
    return velocity_law(jax.random.fold_in(key, 3), CB)


def draw_fine_velocity(key, part):
    return velocity_law(jax.random.fold_in(key, 5), FB)


def source_rows(source_key, forced):
    first, second, third, fourth = jax.random.split(source_key, 4)
    order = jax.random.permutation(first, N_BLOCKS)
    spot = jnp.sum(jnp.arange(N_BLOCKS) * (order == forced).astype(jnp.int32))
    swapped = order.at[spot].set(order[0]).at[0].set(forced)
    doubles = jax.random.randint(second, (), 1, PAIRS_DEV // 2 + 1)
    rotate = jax.random.randint(third, (), 0, 3)
    place = jnp.arange(N_BLOCKS)
    counts = jnp.where(place < doubles, 2, jnp.where(place < PAIRS_DEV - doubles, 1, 0))
    starts = jnp.cumsum(counts) - counts
    rank = jnp.arange(PAIRS_DEV)
    link = jnp.sum((starts[None, :] <= rank[:, None]).astype(jnp.int32), axis=1) - 1
    owner = swapped[link]
    face = (rank + rotate) % 3
    within = rank // 3
    slot_tables = jax.vmap(lambda sub: jax.random.permutation(sub, FB))(jax.random.split(fourth, 3))
    fine_slot = slot_tables[face, within]
    return (owner.astype(jnp.int32), face.astype(jnp.int32), fine_slot.astype(jnp.int32))


def one_group(group_key):
    first, second, third, fourth = jax.random.split(group_key, 4)
    forced = jax.random.randint(first, (), 0, N_BLOCKS)
    owner, face, fine_slot = jax.vmap(lambda sub: source_rows(sub, forced))(jax.random.split(second, N_BLOCKS))
    target = owner * 3 + face
    hits = jnp.sum((target[:, :, None] == jnp.arange(N_BLOCKS * 3)[None, None, :]).astype(jnp.int32), axis=1)
    before = jnp.cumsum(hits, axis=0) - hits
    index = jnp.take_along_axis(before, target, axis=1)
    key_tables = jax.vmap(lambda sub: jax.random.permutation(sub, 4 * CB))(jax.random.split(third, N_BLOCKS * 3))
    value = key_tables[target, index]
    columns = jnp.stack([fine_slot, face, owner, value // 4, value // 2 % 2, value % 2], axis=-1)
    orders = jax.vmap(lambda sub: jax.random.permutation(sub, PAIRS_DEV))(jax.random.split(fourth, N_BLOCKS))
    shuffled = jnp.take_along_axis(columns, orders[:, :, None], axis=1)
    return shuffled.reshape(N_BLOCKS * PAIRS_DEV, 6).astype(jnp.int32)


def draw_pairs(key, part):
    base = jax.random.fold_in(key, 11)
    group_keys = jax.vmap(lambda index: jax.random.fold_in(base, index))(jnp.arange(N_GZ))
    return jax.vmap(one_group)(group_keys)


def block_scale(rng, dims, shards, smallest, top_value):
    level, own = 1.0, jax.random.fold_in(rng, 6)
    for dim, parts in shards:
        heights = jnp.exp(jax.random.uniform(jax.random.fold_in(own, dim), (parts,), jnp.float32, smallest / len(shards), top_value / len(shards)))
        level = level * jnp.repeat(heights, dims[dim] // parts).reshape([-1 if axis == dim else 1 for axis in range(len(dims))])
    return level


def gaussian(rng, extent, deviation, reach, shards=(), kind=jnp.bfloat16):
    result = jax.random.normal(rng, extent, jnp.float32) * deviation
    if len(shards) > 0:
        result = block_scale(rng, extent, shards, -0.22, 0.18) * result
    return jnp.clip(result, min=-reach, max=reach).astype(kind)


def setup_inputs(seed: int = 0) -> dict:
    seeds = jax.random.split(jax.random.key(seed), 6)
    coarse_field = gaussian(seeds[0], (N_GZ, COARSE_ALL, 3, EDGE ** 3), 1.0, 6.0, ((0, 4), (1, 8)), jnp.float32)
    coarse_velocity = draw_coarse_velocity(jax.random.fold_in(seeds[5], 71), 0)
    fine_field = gaussian(seeds[2], (N_GZ, FINE_ALL, 3, EDGE ** 3), 1.0, 6.0, ((0, 4), (1, 8)), jnp.float32)
    fine_velocity = draw_fine_velocity(jax.random.fold_in(seeds[5], 71), 0)
    pairs = draw_pairs(jax.random.fold_in(seeds[5], 71), 0)
    return dict(coarse_field=coarse_field, coarse_velocity=coarse_velocity, fine_field=fine_field, fine_velocity=fine_velocity, pairs=pairs)


TANGENT = ((1, 2), (0, 2), (0, 1))

def cube(values):
    return values.reshape(values.shape[:-1] + (EDGE, EDGE, EDGE))

def centred(field):
    return [0.5 * (field[along] + jnp.roll(field[along], -1, axis=along)) for along in range(3)]

def cell_speed(field, velocity):
    centre = centred(field)
    speed_v = jnp.sqrt(velocity[0] * velocity[0] + velocity[1] * velocity[1] + velocity[2] * velocity[2])
    speed_b = jnp.sqrt(centre[0] * centre[0] + centre[1] * centre[1] + centre[2] * centre[2])
    return jnp.max(speed_v + speed_b)

def edge_fields(field, velocity):
    field_x, field_y, field_z = centred(field)
    vel_x, vel_y, vel_z = (velocity[0], velocity[1], velocity[2])
    cell_x = -(vel_y * field_z - vel_z * field_y)
    cell_y = -(vel_z * field_x - vel_x * field_z)
    cell_z = -(vel_x * field_y - vel_y * field_x)

    def corner(values, first, second):
        rolled = jnp.roll(values, 1, axis=first)
        return 0.25 * (values + rolled + jnp.roll(values, 1, axis=second) + jnp.roll(rolled, 1, axis=second))
    return [corner(cell_x, 1, 2), corner(cell_y, 0, 2), corner(cell_z, 0, 1)]

def faraday(field, emf, factor):

    def ahead(values, along):
        return jnp.roll(values, -1, axis=along) - values
    emf_x, emf_y, emf_z = emf
    new_x = field[0] - factor * (ahead(emf_z, 1) - ahead(emf_y, 2))
    new_y = field[1] - factor * (ahead(emf_x, 2) - ahead(emf_z, 0))
    new_z = field[2] - factor * (ahead(emf_y, 0) - ahead(emf_x, 1))
    return jnp.stack([new_x, new_y, new_z])

def put_plane(values, normal, plane_new):
    shape = [1, 1, 1]
    shape[normal] = EDGE
    first = (jnp.arange(EDGE) == 0).reshape(shape)
    return jnp.where(first, jnp.expand_dims(plane_new, normal), values)

def restrict(planes):
    first = 0.5 * (planes[:, 0, 0::2, 0::2] + planes[:, 0, 1::2, 0::2])
    second = 0.5 * (planes[:, 1, 0::2, 0::2] + planes[:, 1, 0::2, 1::2])
    return jnp.stack([first, second], axis=1)

def reference(coarse_field, coarse_velocity, fine_field, fine_velocity, pairs):
    coarse_flat = coarse_field.reshape(-1, 3, EDGE ** 3)
    coarse_vel = coarse_velocity.reshape(-1, 3, EDGE ** 3)
    fine_flat = fine_field.reshape(-1, 3, EDGE ** 3)
    fine_vel = fine_velocity.reshape(-1, 3, EDGE ** 3)
    speeds_c = lax.map(lambda item: cell_speed(cube(item[0]), cube(item[1])), (coarse_flat, coarse_vel))
    speeds_f = lax.map(lambda item: cell_speed(cube(item[0]), cube(item[1])), (fine_flat, fine_vel))
    top_speed = jnp.maximum(jnp.max(speeds_c), jnp.max(speeds_f))
    time_step = 0.2 / top_speed

    def fine_step(item):
        field = cube(item[0])
        emf = edge_fields(field, cube(item[1]))
        updated = faraday(field, emf, time_step / 0.5)
        tangents = jnp.stack([jnp.stack([jnp.take(emf[TANGENT[normal][0]], 0, axis=normal), jnp.take(emf[TANGENT[normal][1]], 0, axis=normal)]) for normal in range(3)])
        normals = jnp.stack([jnp.take(updated[normal], 0, axis=normal) for normal in range(3)])
        return (updated.reshape(3, EDGE ** 3), tangents, normals)
    fine_out, fine_tangents, fine_normals = lax.map(fine_step, (fine_flat, fine_vel))
    pair_rows = pairs.reshape(-1, 6).astype(jnp.int32)
    count = pair_rows.shape[0]
    group = (jnp.arange(count, dtype=jnp.int32) // (PAIRS_DEV * N_BLOCKS)).astype(jnp.int32)
    source = (jnp.arange(count, dtype=jnp.int32) % (PAIRS_DEV * N_BLOCKS) // PAIRS_DEV).astype(jnp.int32)
    fine_block = (group * (FB * N_BLOCKS) + source * FB + pair_rows[:, 0]).astype(jnp.int32)
    face_dir = pair_rows[:, 1]
    coarse_block = (group * (CB * N_BLOCKS) + pair_rows[:, 2] * CB + pair_rows[:, 3]).astype(jnp.int32)
    quad_row = pair_rows[:, 4]
    quad_col = pair_rows[:, 5]
    restricted = restrict(fine_tangents[fine_block, face_dir])
    span = jnp.arange(HALF, dtype=jnp.int32)
    rows_idx = (quad_row[:, None, None, None] * HALF + span[None, None, :, None]).astype(jnp.int32)
    cols_idx = (quad_col[:, None, None, None] * HALF + span[None, None, None, :]).astype(jnp.int32)
    comp_idx = jnp.arange(2, dtype=jnp.int32)[None, :, None, None]
    blocks_all = coarse_flat.shape[0]
    replaced = jnp.zeros((blocks_all, 3, 2, EDGE, EDGE), jnp.float32)
    replaced = replaced.at[coarse_block[:, None, None, None], face_dir[:, None, None, None], comp_idx, rows_idx, cols_idx].set(restricted)
    hit_mask = jnp.zeros((blocks_all, 3, EDGE, EDGE), jnp.float32)
    hit_mask = hit_mask.at[coarse_block[:, None, None], face_dir[:, None, None], rows_idx[:, 0], cols_idx[:, 0]].set(jnp.ones((count, HALF, HALF), jnp.float32))

    def coarse_step(item):
        field = cube(item[0])
        emf = edge_fields(field, cube(item[1]))
        for normal in range(3):
            for which in range(2):
                along = TANGENT[normal][which]
                plane_now = jnp.take(emf[along], 0, axis=normal)
                plane_new = jnp.where(item[3][normal] > 0.5, item[2][normal, which], plane_now)
                emf[along] = put_plane(emf[along], normal, plane_new)
        updated = faraday(field, emf, time_step / 1.0)
        normals = jnp.stack([jnp.take(updated[normal], 0, axis=normal) for normal in range(3)])
        return (updated.reshape(3, EDGE ** 3), normals)
    coarse_out, coarse_normals = lax.map(coarse_step, (coarse_flat, coarse_vel, replaced, hit_mask))
    quadrant = coarse_normals[coarse_block[:, None, None], face_dir[:, None, None], rows_idx[:, 0], cols_idx[:, 0]]
    prolonged = jnp.repeat(jnp.repeat(quadrant, 2, axis=1), 2, axis=2)
    face_jump = fine_normals[fine_block, face_dir] - prolonged
    return (coarse_out.reshape(coarse_field.shape), fine_out.reshape(fine_field.shape), face_jump.reshape(N_GZ, PAIRS_DEV * N_BLOCKS, EDGE * EDGE))
```

```python
import functools

import jax
import jax.numpy as jnp
from jax import lax
from jax.experimental import pallas as pl
from jax.experimental.pallas import tpu as pltpu
from jax.sharding import PartitionSpec as P

EDGE = 16
HALF = 8
CAP = 2
LANES = 128
ROWS = 8
TILES = EDGE**3 // LANES
BIG = 1e30
EMPTY = 3e38
TANGENT = ((1, 2), (0, 2), (0, 1))
MESH = pl.DeviceIdType.MESH


def take(values, index):
    return jnp.take_along_axis(values, index, axis=1, mode="promise_in_bounds")


def kernel(
    peers,
    groups,
    coarse_count,
    fine_count,
    pair_count,
    pairs,
    cb_hbm,
    cv_hbm,
    fb_hbm,
    fv_hbm,
    curl_c,
    curl_f,
    step_out,
    jump_out,
    cb,
    cv,
    fb,
    fv,
    emf_c,
    emf_f,
    tab_r,
    tab_n,
    rep,
    own,
    picked,
    send1,
    recv1,
    send2,
    recv2,
    gmax,
    gmax_in,
    load_sem,
    s1_sem,
    r1_sem,
    s2_sem,
    r2_sem,
    sg_sem,
    rg_sem,
):
    me = lax.axis_index("blocks")
    mg = lax.axis_index("gz")
    few = peers <= 8

    def each_peer(body):
        lax.fori_loop(1, peers, lambda k, _: (body(lax.rem(me + k, peers)), 0)[1], 0, unroll=few)

    def each_group(body):
        for k in range(1, groups):
            body(lax.rem(mg + k, groups))

    loads = [
        pltpu.make_async_copy(src, dst, load_sem.at[n])
        for n, (src, dst) in enumerate(((fb_hbm, fb), (fv_hbm, fv), (cb_hbm, cb), (cv_hbm, cv)))
    ]
    for load in loads:
        load.start()
    barrier = pltpu.get_barrier_semaphore()
    each_peer(
        lambda p: pl.semaphore_signal(barrier, inc=1, device_id=(p, mg), device_id_type=MESH)
    )
    each_group(
        lambda g: pl.semaphore_signal(barrier, inc=1, device_id=(me, g), device_id_type=MESH)
    )

    lane = lax.broadcasted_iota(jnp.int32, (ROWS, LANES), 1)
    sub = lax.broadcasted_iota(jnp.int32, (ROWS, LANES), 0)
    k_of = lane % EDGE
    first_y = lane < EDGE
    last_y = lane >= LANES - EDGE
    first_z = k_of == 0
    last_z = k_of == EDGE - 1

    def back_y(pair):
        low, high = pltpu.roll(pair[0], EDGE, 1), pltpu.roll(pair[1], EDGE, 1)
        return jnp.where(first_y, high, low), jnp.where(first_y, low, high)

    def ahead_y(pair):
        low, high = pltpu.roll(pair[0], LANES - EDGE, 1), pltpu.roll(pair[1], LANES - EDGE, 1)
        return jnp.where(last_y, high, low), jnp.where(last_y, low, high)

    def back_z(pair):
        return tuple(
            jnp.where(first_z, pltpu.roll(v, LANES - EDGE + 1, 1), pltpu.roll(v, 1, 1))
            for v in pair
        )

    def ahead_z(pair):
        return tuple(
            jnp.where(last_z, pltpu.roll(v, EDGE - 1, 1), pltpu.roll(v, LANES - 1, 1))
            for v in pair
        )

    def add(a, b):
        return a[0] + b[0], a[1] + b[1]

    def sub2(a, b):
        return a[0] - b[0], a[1] - b[1]

    def mul(a, b):
        return a[0] * b[0], a[1] * b[1]

    def scale(s, a):
        return s * a[0], s * a[1]

    def column(tile):
        return pl.ds(pl.multiple_of(tile * LANES, LANES), LANES)

    def blocked(ref, g):
        def read(c, i):
            return tuple(ref[c, ROWS * g : ROWS * g + ROWS, column(2 * i + h)] for h in range(2))

        return read

    def strided(ref, start):
        def read(c, i):
            return tuple(
                ref[pl.ds(start * 3 * TILES + c * TILES + 2 * i + h, ROWS, stride=3 * TILES), :]
                for h in range(2)
            )

        return read

    def blocked_put(ref, g):
        def put(c, i, pair):
            for h in range(2):
                ref[c, ROWS * g : ROWS * g + ROWS, column(2 * i + h)] = pair[h]

        return put

    def strided_put(ref, start):
        def put(c, i, pair):
            for h in range(2):
                ref[pl.ds(start * 3 * TILES + c * TILES + 2 * i + h, ROWS, stride=3 * TILES), :] = (
                    pair[h]
                )

        return put

    def cells(field, velocity, i, want_speed):
        after = lax.rem(i + 1, EDGE)
        b_x, b_y, b_z = field(0, i), field(1, i), field(2, i)
        c_x = scale(0.5, add(b_x, field(0, after)))
        c_y = scale(0.5, add(b_y, ahead_y(b_y)))
        c_z = scale(0.5, add(b_z, ahead_z(b_z)))
        v_x, v_y, v_z = velocity(0, i), velocity(1, i), velocity(2, i)
        cell_y = sub2(mul(v_x, c_z), mul(v_z, c_x))
        cell_z = sub2(mul(v_y, c_x), mul(v_x, c_y))
        part_y = scale(0.25, add(cell_y, back_z(cell_y)))
        part_z = scale(0.25, add(cell_z, back_y(cell_z)))
        if not want_speed:
            return part_y, part_z
        cell_x = sub2(mul(v_z, c_y), mul(v_y, c_z))
        part_x = scale(0.25, add(cell_x, back_y(cell_x)))
        e_x = add(part_x, back_z(part_x))
        vv = add(add(mul(v_x, v_x), mul(v_y, v_y)), mul(v_z, v_z))
        cc = add(add(mul(c_x, c_x), mul(c_y, c_y)), mul(c_z, c_z))
        speed = jnp.maximum(
            jnp.sqrt(vv[0]) + jnp.sqrt(cc[0]), jnp.sqrt(vv[1]) + jnp.sqrt(cc[1])
        )
        return part_y, part_z, e_x, speed

    def emf_pass(sources, target, best):
        starts = [cells(f, v, EDGE - 1, False) for f, v in sources]

        def step(i, carry):
            parts, top = carry
            fresh = []
            for g, (f, v) in enumerate(sources):
                part_y, part_z, e_x, speed = cells(f, v, i, True)
                put = blocked_put(target, g)
                put(0, i, e_x)
                put(1, i, add(part_y, parts[g][0]))
                put(2, i, add(part_z, parts[g][1]))
                top = jnp.maximum(top, speed)
                fresh.append((part_y, part_z))
            return fresh, top

        return lax.fori_loop(0, EDGE, step, (starts, best))[1]

    def curl_pass(emf, puts):
        def step(i, carry):
            after = lax.rem(i + 1, EDGE)
            for g, put in enumerate(puts):
                read = blocked(emf, g)
                e_x, e_y, e_z = read(0, i), read(1, i), read(2, i)
                put(0, i, sub2(sub2(ahead_y(e_z), e_z), sub2(ahead_z(e_y), e_y)))
                put(1, i, sub2(sub2(ahead_z(e_x), e_x), sub2(read(2, after), e_z)))
                put(2, i, sub2(sub2(read(1, after), e_y), sub2(ahead_y(e_x), e_x)))
            return carry

        lax.fori_loop(0, EDGE, step, 0)

    coarse_groups = coarse_count // ROWS
    fine_groups = -(-fine_count // ROWS)
    fine_starts = [min(ROWS * g, fine_count - ROWS) for g in range(fine_groups)]
    fine_rows = ROWS * fine_groups

    def fine_row(slot):
        last = ROWS * (fine_groups - 1)
        return jnp.where(slot < last, slot, slot - fine_starts[-1] + last)

    loads[0].wait()
    loads[1].wait()
    best = emf_pass([(strided(fb, s), strided(fv, s)) for s in fine_starts], emf_f, jnp.zeros((ROWS, LANES), jnp.float32))

    within = lane % 64
    row_m, col_n = within // HALF, within % HALF
    face_x = (row_m % 4) * 32 + col_n * 2
    for g in range(fine_groups):
        read = blocked(emf_f, g)
        for d in range(3):
            kept = []
            for which in range(2):
                axis = TANGENT[d][which]
                acc = jnp.zeros((ROWS, LANES), jnp.float32)
                if d == 0:
                    pair = read(axis, 0)
                    shift = EDGE if which == 0 else 1
                    for h in range(2):
                        mean = 0.5 * (pair[h] + pltpu.roll(pair[h], LANES - shift, 1))
                        acc = jnp.where(row_m // 4 == h, take(mean, face_x), acc)
                elif d == 1:
                    for m in range(HALF):
                        here = read(axis, 2 * m)[0]
                        other = read(axis, 2 * m + 1)[0] if which == 0 else pltpu.roll(here, LANES - 1, 1)
                        acc = jnp.where(row_m == m, take(0.5 * (here + other), col_n * 2), acc)
                else:
                    for m in range(HALF):
                        here = read(axis, 2 * m)
                        other = read(axis, 2 * m + 1) if which == 0 else [pltpu.roll(v, LANES - EDGE, 1) for v in here]
                        for h in range(2):
                            got = take(0.5 * (here[h] + other[h]), (col_n % 4) * 32)
                            acc = jnp.where((row_m == m) & (col_n // 4 == h), got, acc)
                kept.append(acc)
            tab_r[d * fine_rows + ROWS * g : d * fine_rows + ROWS * g + ROWS, :] = jnp.where(
                lane < 64, kept[0], kept[1]
            )

    slot_of = [pairs[r, 0] for r in range(pair_count)]
    face_of = [pairs[r, 1] for r in range(pair_count)]
    owner_of = [pairs[r, 2] for r in range(pair_count)]
    table_row = [face_of[r] * fine_rows + fine_row(slot_of[r]) for r in range(pair_count)]
    message_row = []
    for r in range(pair_count):
        rank = jnp.int32(0)
        for q in range(r):
            rank = rank + jnp.where(owner_of[q] == owner_of[r], 1, 0)
        message_row.append(owner_of[r] * ROWS + rank)

    box = lax.broadcasted_iota(jnp.int32, (peers * ROWS, LANES), 0)
    message = jnp.full((peers * ROWS, LANES), -1.0, jnp.float32)
    for r in range(pair_count):
        code = pairs[r, 3] * 12 + face_of[r] * 4 + pairs[r, 4] * 2 + pairs[r, 5]
        values = tab_r[pl.ds(table_row[r], 1), :]
        message = jnp.where(box == message_row[r], values, message)
        message = jnp.where(box == message_row[r] + CAP, code.astype(jnp.float32), message)
    send1[...] = message

    pl.semaphore_wait(barrier, peers - 1 + groups - 1)

    def slot(ref, p):
        return ref.at[pl.ds(pl.multiple_of(p * ROWS, ROWS), ROWS)]

    def out1(p):
        return pltpu.make_async_remote_copy(
            src_ref=slot(send1, p), dst_ref=slot(recv1, me), send_sem=s1_sem.at[p],
            recv_sem=r1_sem.at[me], device_id=(p, mg), device_id_type=MESH,
        )

    def in1(p):
        return pltpu.make_async_remote_copy(
            src_ref=slot(send1, p), dst_ref=slot(recv1, p), send_sem=s1_sem.at[p],
            recv_sem=r1_sem.at[p], device_id=(p, mg), device_id_type=MESH,
        )

    def out2(p):
        return pltpu.make_async_remote_copy(
            src_ref=slot(send2, p), dst_ref=slot(recv2, me), send_sem=s2_sem.at[p],
            recv_sem=r2_sem.at[me], device_id=(p, mg), device_id_type=MESH,
        )

    def in2(p):
        return pltpu.make_async_remote_copy(
            src_ref=slot(send2, p), dst_ref=slot(recv2, p), send_sem=s2_sem.at[p],
            recv_sem=r2_sem.at[p], device_id=(p, mg), device_id_type=MESH,
        )

    def outg(g):
        return pltpu.make_async_remote_copy(
            src_ref=gmax, dst_ref=slot(gmax_in, mg), send_sem=sg_sem.at[g],
            recv_sem=rg_sem.at[mg], device_id=(me, g), device_id_type=MESH,
        )

    def ing(g):
        return pltpu.make_async_remote_copy(
            src_ref=gmax, dst_ref=slot(gmax_in, g), send_sem=sg_sem.at[g],
            recv_sem=rg_sem.at[g], device_id=(me, g), device_id_type=MESH,
        )

    each_peer(lambda p: out1(p).start())

    loads[2].wait()
    loads[3].wait()
    best = emf_pass([(blocked(cb, g), blocked(cv, g)) for g in range(coarse_groups)], emf_c, best)
    gmax[...] = best
    each_group(lambda g: outg(g).start())

    curl_pass(emf_f, [strided_put(curl_f, s) for s in fine_starts])

    slot(recv1, me)[...] = slot(send1, me)[...]
    each_peer(lambda p: in1(p).wait_recv())
    codes = [
        [((sub + ROWS * g) * 12 + dq).astype(jnp.float32) for dq in range(12)]
        for g in range(coarse_groups)
    ]

    def row_of(ref, n):
        return jnp.broadcast_to(ref[pl.ds(n, 1), :], (ROWS, LANES))

    def collect(p, held):
        for c in range(CAP):
            values, key = row_of(recv1, p * ROWS + c), row_of(recv1, p * ROWS + CAP + c)
            held = [
                [jnp.where(key == codes[g][dq], values, held[g][dq]) for dq in range(12)]
                for g in range(coarse_groups)
            ]
        return held

    empty = jnp.full((ROWS, LANES), EMPTY, jnp.float32)
    held = lax.fori_loop(0, peers, collect, [[empty] * 12 for _ in range(coarse_groups)])
    halves = k_of < HALF
    for g in range(coarse_groups):
        def patch(axis, tile, value, mask):
            where = (axis, slice(ROWS * g, ROWS * g + ROWS), slice(tile * LANES, tile * LANES + LANES))
            put = value < BIG
            if mask is not None:
                put = put & mask
            emf_c[where] = jnp.where(put, value, emf_c[where])

        for d in range(3):
            for which in range(2):
                axis = TANGENT[d][which]
                for q1 in range(2):
                    low, high = held[g][d * 4 + q1 * 2], held[g][d * 4 + q1 * 2 + 1]
                    if d < 2:
                        spread = (lane // EDGE) * HALF + lane % HALF + 64 * which
                        both = jnp.where(halves, take(low, spread), take(high, spread))
                        if d == 0:
                            patch(axis, q1, both, None)
                        else:
                            for m in range(HALF):
                                turned = both if m == 0 else pltpu.roll(both, LANES - EDGE * m, 1)
                                patch(axis, 2 * (q1 * HALF + m), turned, first_y)
                    else:
                        for m in range(HALF):
                            for q2 in range(2):
                                got = take((low, high)[q2], m * HALF + lane // EDGE + 64 * which)
                                patch(axis, 2 * (q1 * HALF + m) + q2, got, first_z)

    curl_pass(emf_c, [blocked_put(curl_c, g) for g in range(coarse_groups)])

    def gathered_rows(read, d, h):
        out = jnp.zeros((ROWS, LANES), jnp.float32)
        for m in range(HALF):
            here = read(d, h * HALF + m)[0]
            out = jnp.where(lane // EDGE == m, here if m == 0 else pltpu.roll(here, EDGE * m, 1), out)
        return out

    for g in range(coarse_groups):
        reads = (blocked(cb, g), blocked(curl_c, g))
        for d in range(3):
            for q1 in range(2):
                if d == 0:
                    faces = [read(0, 0)[q1] for read in reads]
                elif d == 1:
                    faces = [gathered_rows(read, 1, q1) for read in reads]
                for q2 in range(2):
                    if d < 2:
                        index = row_m * EDGE + q2 * HALF + col_n
                        quads = [take(face, index) for face in faces]
                    else:
                        quads = []
                        for read in reads:
                            acc = jnp.zeros((ROWS, LANES), jnp.float32)
                            for m in range(HALF):
                                acc = jnp.where(
                                    row_m == m, take(read(2, q1 * HALF + m)[q2], col_n * EDGE), acc
                                )
                            quads.append(acc)
                    rep[(g * 12 + d * 4 + q1 * 2 + q2) * ROWS : (g * 12 + d * 4 + q1 * 2 + q2 + 1) * ROWS, :] = (
                        jnp.where(lane < 64, quads[0], quads[1])
                    )

    each_group(lambda g: ing(g).wait_recv())
    for k in range(1, groups):
        best = jnp.maximum(best, slot(gmax_in, lax.rem(mg + k, groups))[...])
    top_row = jnp.max(best, axis=0, keepdims=True)

    def answer(p, carry):
        rows = jnp.broadcast_to(top_row, (ROWS, LANES))
        for c in range(CAP):
            key = row_of(recv1, p * ROWS + CAP + c)
            acc = jnp.zeros((ROWS, LANES), jnp.float32)
            for g in range(coarse_groups):
                for dq in range(12):
                    acc = jnp.where(
                        key == codes[g][dq],
                        rep[(g * 12 + dq) * ROWS : (g * 12 + dq + 1) * ROWS, :],
                        acc,
                    )
            rows = jnp.where(sub == c, jnp.sum(acc, axis=0, keepdims=True), rows)
        slot(send2, p)[...] = rows
        return carry

    lax.fori_loop(0, peers, answer, 0)
    each_peer(lambda p: out2(p).start())

    for g in range(fine_groups):
        for n, read in enumerate((strided(fb, fine_starts[g]), strided(curl_f, fine_starts[g]))):
            for d in range(3):
                for h in range(2):
                    if d == 0:
                        face = read(0, 0)[h]
                    elif d == 1:
                        face = gathered_rows(read, 1, h)
                    else:
                        face = jnp.zeros((ROWS, LANES), jnp.float32)
                        for m in range(HALF):
                            pair = read(2, h * HALF + m)
                            for part in range(2):
                                face = jnp.where(
                                    (lane // EDGE == m) & (k_of // HALF == part),
                                    take(pair[part], (lane % HALF) * EDGE),
                                    face,
                                )
                    tab_n[
                        d * fine_rows + ROWS * g : d * fine_rows + ROWS * g + ROWS,
                        (2 * n + h) * LANES : (2 * n + h + 1) * LANES,
                    ] = face
    for r in range(pair_count):
        picked[r : r + 1, :] = tab_n[pl.ds(table_row[r], 1), :]

    slot(recv2, me)[...] = slot(send2, me)[...]
    each_peer(lambda p: in2(p).wait_recv())
    top = jnp.full((ROWS, LANES), 0.0, jnp.float32)
    top = lax.fori_loop(0, peers, lambda p, t: jnp.maximum(t, row_of(recv2, p * ROWS + CAP)), top)
    dt = 0.2 / jnp.max(top, axis=1, keepdims=True)
    step_out[...] = jnp.broadcast_to(dt, (ROWS, LANES))
    for r in range(pair_count):
        own[r : r + 1, :] = recv2[pl.ds(message_row[r], 1), :]
    for s in range(0, pair_count, ROWS):
        take_rows = min(ROWS, pair_count - s)
        quad = own[s : s + ROWS, :]
        quad = quad - dt * pltpu.roll(quad, 64, 1)
        for h in range(2):
            coarse = take(quad, (4 * h + lane // 32) * HALF + k_of // 2)
            fine = picked[s : s + ROWS, h * LANES : (h + 1) * LANES] - (dt / 0.5) * picked[
                s : s + ROWS, (2 + h) * LANES : (3 + h) * LANES
            ]
            jump_out[s : s + take_rows, h * LANES : (h + 1) * LANES] = (fine - coarse)[:take_rows]

    each_peer(lambda p: out1(p).wait_send())
    each_peer(lambda p: out2(p).wait_send())
    each_group(lambda g: outg(g).wait_send())


def on_device(peers, groups, coarse_field, coarse_velocity, fine_field, fine_velocity, pairs):
    coarse_count, fine_count = coarse_field.shape[1], fine_field.shape[1]
    pair_count = pairs.shape[1]
    cells = EDGE**3
    flat_rows = fine_count * 3 * TILES

    def coarse_view(x):
        return jnp.transpose(x[0], (1, 0, 2))

    def fine_view(x):
        return x.reshape(flat_rows, LANES)

    fine_rows = ROWS * -(-fine_count // ROWS)
    pair_rows = ROWS * -(-pair_count // ROWS)
    cb, cv = coarse_view(coarse_field), coarse_view(coarse_velocity)
    fb, fv = fine_view(fine_field), fine_view(fine_velocity)
    f32 = jnp.float32
    dma = pltpu.SemaphoreType.DMA
    vmem = pltpu.VMEM
    anywhere = pl.BlockSpec(memory_space=pl.ANY)
    inside = pl.BlockSpec(memory_space=pltpu.VMEM)
    coarse_shape, fine_shape = (3, coarse_count, cells), (flat_rows, LANES)
    curl_c, curl_f, step, jump = pl.pallas_call(
        functools.partial(kernel, peers, groups, coarse_count, fine_count, pair_count),
        out_shape=(
            jax.ShapeDtypeStruct(coarse_shape, f32),
            jax.ShapeDtypeStruct(fine_shape, f32),
            jax.ShapeDtypeStruct((ROWS, LANES), f32),
            jax.ShapeDtypeStruct((pair_count, EDGE * EDGE), f32),
        ),
        in_specs=[pl.BlockSpec(memory_space=pltpu.SMEM)] + [anywhere] * 4,
        out_specs=(inside,) * 4,
        scratch_shapes=[
            vmem(coarse_shape, f32),
            vmem(coarse_shape, f32),
            vmem(fine_shape, f32),
            vmem(fine_shape, f32),
            vmem(coarse_shape, f32),
            vmem((3, fine_rows, cells), f32),
            vmem((3 * fine_rows, LANES), f32),
            vmem((3 * fine_rows, 4 * LANES), f32),
            vmem((12 * coarse_count, LANES), f32),
            vmem((pair_rows, LANES), f32),
            vmem((pair_rows, 4 * LANES), f32),
            vmem((peers * ROWS, LANES), f32),
            vmem((peers * ROWS, LANES), f32),
            vmem((peers * ROWS, LANES), f32),
            vmem((peers * ROWS, LANES), f32),
            vmem((ROWS, LANES), f32),
            vmem((groups * ROWS, LANES), f32),
            dma((4,)),
            dma((peers,)),
            dma((peers,)),
            dma((peers,)),
            dma((peers,)),
            dma((groups,)),
            dma((groups,)),
        ],
        compiler_params=pltpu.CompilerParams(
            collective_id=0, has_side_effects=True, vmem_limit_bytes=32 * 1024 * 1024
        ),
    )(pairs[0], cb, cv, fb, fv)
    dt = step[0, 0]
    coarse_out = cb - dt * curl_c
    fine_out = fb - (dt / 0.5) * curl_f
    return (
        jnp.transpose(coarse_out, (1, 0, 2))[None],
        fine_out.reshape(1, fine_count, 3, cells),
        jump[None],
    )


def solution(mesh):
    spec = P("gz", "blocks", None, None)
    flat = P("gz", "blocks", None)
    return jax.shard_map(
        functools.partial(on_device, mesh.shape["blocks"], mesh.shape["gz"]),
        mesh=mesh,
        in_specs=(spec, spec, spec, spec, flat),
        out_specs=(spec, spec, flat),
        check_vma=False,
    )
```

```python
import functools

import jax
import jax.numpy as jnp
from jax import lax
from jax.experimental import pallas as pl
from jax.experimental.pallas import tpu as pltpu
from jax.sharding import PartitionSpec as P

EDGE = 16
HALF = 8
CAP = 2
LANES = 128
ROWS = 8
TILES = EDGE**3 // LANES
BIG = 1e30
EMPTY = 3e38
TANGENT = ((1, 2), (0, 2), (0, 1))
MESH = pl.DeviceIdType.MESH


def take(values, index):
    return jnp.take_along_axis(values, index, axis=1, mode="promise_in_bounds")


def kernel(
    peers,
    groups,
    coarse_count,
    fine_count,
    pair_count,
    pairs_hbm,
    cb_hbm,
    cv_hbm,
    fb_hbm,
    fv_hbm,
    curl_c,
    curl_f,
    jump_out,
    pairs,
    cb,
    cv,
    fb,
    fv,
    emf_c,
    emf_f,
    tab_r,
    tab_n,
    rep,
    own,
    picked,
    send1,
    recv1,
    send2,
    recv2,
    gmax,
    gmax_in,
    load_sem,
    s1_sem,
    r1_sem,
    s2_sem,
    r2_sem,
    sg_sem,
    rg_sem,
):
    me = lax.axis_index("blocks")
    mg = lax.axis_index("gz")
    few = peers <= 8

    def each_peer(body):
        lax.fori_loop(1, peers, lambda k, _: (body(lax.rem(me + k, peers)), 0)[1], 0, unroll=few)

    def each_group(body):
        for k in range(1, groups):
            body(lax.rem(mg + k, groups))

    loads = [
        pltpu.make_async_copy(src, dst, load_sem.at[n])
        for n, (src, dst) in enumerate(((fb_hbm, fb), (fv_hbm, fv), (cb_hbm, cb), (cv_hbm, cv)))
    ]
    listed = pltpu.make_async_copy(pairs_hbm, pairs, load_sem.at[4])
    listed.start()
    for load in loads:
        load.start()
    barrier = pltpu.get_barrier_semaphore()
    each_peer(
        lambda p: pl.semaphore_signal(barrier, inc=1, device_id=(p, mg), device_id_type=MESH)
    )
    each_group(
        lambda g: pl.semaphore_signal(barrier, inc=1, device_id=(me, g), device_id_type=MESH)
    )

    lane = lax.broadcasted_iota(jnp.int32, (ROWS, LANES), 1)
    sub = lax.broadcasted_iota(jnp.int32, (ROWS, LANES), 0)
    k_of = lane % EDGE
    first_y = lane < EDGE
    last_y = lane >= LANES - EDGE
    first_z = k_of == 0
    last_z = k_of == EDGE - 1

    def back_y(pair):
        low, high = pltpu.roll(pair[0], EDGE, 1), pltpu.roll(pair[1], EDGE, 1)
        return jnp.where(first_y, high, low), jnp.where(first_y, low, high)

    def ahead_y(pair):
        low, high = pltpu.roll(pair[0], LANES - EDGE, 1), pltpu.roll(pair[1], LANES - EDGE, 1)
        return jnp.where(last_y, high, low), jnp.where(last_y, low, high)

    def back_z(pair):
        return tuple(
            jnp.where(first_z, pltpu.roll(v, LANES - EDGE + 1, 1), pltpu.roll(v, 1, 1))
            for v in pair
        )

    def ahead_z(pair):
        return tuple(
            jnp.where(last_z, pltpu.roll(v, EDGE - 1, 1), pltpu.roll(v, LANES - 1, 1))
            for v in pair
        )

    def add(a, b):
        return a[0] + b[0], a[1] + b[1]

    def sub2(a, b):
        return a[0] - b[0], a[1] - b[1]

    def mul(a, b):
        return a[0] * b[0], a[1] * b[1]

    def scale(s, a):
        return s * a[0], s * a[1]

    def column(tile):
        return pl.ds(pl.multiple_of(tile * LANES, LANES), LANES)

    def blocked(ref, g):
        def read(c, i):
            return tuple(ref[c, ROWS * g : ROWS * g + ROWS, column(2 * i + h)] for h in range(2))

        return read

    def strided(ref, start):
        def read(c, i):
            return tuple(
                ref[pl.ds(start * 3 * TILES + c * TILES + 2 * i + h, ROWS, stride=3 * TILES), :]
                for h in range(2)
            )

        return read

    def blocked_put(ref, g):
        def put(c, i, pair):
            for h in range(2):
                ref[c, ROWS * g : ROWS * g + ROWS, column(2 * i + h)] = pair[h]

        return put

    def strided_put(ref, start):
        def put(c, i, pair):
            for h in range(2):
                ref[pl.ds(start * 3 * TILES + c * TILES + 2 * i + h, ROWS, stride=3 * TILES), :] = (
                    pair[h]
                )

        return put

    def cells(field, velocity, i, want_speed):
        after = lax.rem(i + 1, EDGE)
        b_x, b_y, b_z = field(0, i), field(1, i), field(2, i)
        c_x = scale(0.5, add(b_x, field(0, after)))
        c_y = scale(0.5, add(b_y, ahead_y(b_y)))
        c_z = scale(0.5, add(b_z, ahead_z(b_z)))
        v_x, v_y, v_z = velocity(0, i), velocity(1, i), velocity(2, i)
        cell_y = sub2(mul(v_x, c_z), mul(v_z, c_x))
        cell_z = sub2(mul(v_y, c_x), mul(v_x, c_y))
        part_y = scale(0.25, add(cell_y, back_z(cell_y)))
        part_z = scale(0.25, add(cell_z, back_y(cell_z)))
        if not want_speed:
            return part_y, part_z
        cell_x = sub2(mul(v_z, c_y), mul(v_y, c_z))
        part_x = scale(0.25, add(cell_x, back_y(cell_x)))
        e_x = add(part_x, back_z(part_x))
        vv = add(add(mul(v_x, v_x), mul(v_y, v_y)), mul(v_z, v_z))
        cc = add(add(mul(c_x, c_x), mul(c_y, c_y)), mul(c_z, c_z))
        speed = jnp.maximum(
            jnp.sqrt(vv[0]) + jnp.sqrt(cc[0]), jnp.sqrt(vv[1]) + jnp.sqrt(cc[1])
        )
        return part_y, part_z, e_x, speed

    def emf_pass(sources, target, best):
        starts = [cells(f, v, EDGE - 1, False) for f, v in sources]

        def step(i, carry):
            parts, top = carry
            fresh = []
            for g, (f, v) in enumerate(sources):
                part_y, part_z, e_x, speed = cells(f, v, i, True)
                put = blocked_put(target, g)
                put(0, i, e_x)
                put(1, i, add(part_y, parts[g][0]))
                put(2, i, add(part_z, parts[g][1]))
                top = jnp.maximum(top, speed)
                fresh.append((part_y, part_z))
            return fresh, top

        return lax.fori_loop(0, EDGE, step, (starts, best))[1]

    def curl_pass(emf, puts):
        def step(i, carry):
            after = lax.rem(i + 1, EDGE)
            for g, put in enumerate(puts):
                read = blocked(emf, g)
                e_x, e_y, e_z = read(0, i), read(1, i), read(2, i)
                put(0, i, sub2(sub2(ahead_y(e_z), e_z), sub2(ahead_z(e_y), e_y)))
                put(1, i, sub2(sub2(ahead_z(e_x), e_x), sub2(read(2, after), e_z)))
                put(2, i, sub2(sub2(read(1, after), e_y), sub2(ahead_y(e_x), e_x)))
            return carry

        lax.fori_loop(0, EDGE, step, 0)

    coarse_groups = coarse_count // ROWS
    fine_groups = -(-fine_count // ROWS)
    fine_starts = [min(ROWS * g, fine_count - ROWS) for g in range(fine_groups)]
    fine_rows = ROWS * fine_groups

    def fine_row(slot):
        last = ROWS * (fine_groups - 1)
        return jnp.where(slot < last, slot, slot - fine_starts[-1] + last)

    loads[0].wait()
    loads[1].wait()
    best = emf_pass([(strided(fb, s), strided(fv, s)) for s in fine_starts], emf_f, jnp.zeros((ROWS, LANES), jnp.float32))

    within = lane % 64
    row_m, col_n = within // HALF, within % HALF
    face_x = (row_m % 4) * 32 + col_n * 2
    for g in range(fine_groups):
        read = blocked(emf_f, g)
        for d in range(3):
            kept = []
            for which in range(2):
                axis = TANGENT[d][which]
                acc = jnp.zeros((ROWS, LANES), jnp.float32)
                if d == 0:
                    pair = read(axis, 0)
                    shift = EDGE if which == 0 else 1
                    for h in range(2):
                        mean = 0.5 * (pair[h] + pltpu.roll(pair[h], LANES - shift, 1))
                        acc = jnp.where(row_m // 4 == h, take(mean, face_x), acc)
                elif d == 1:
                    for m in range(HALF):
                        here = read(axis, 2 * m)[0]
                        other = read(axis, 2 * m + 1)[0] if which == 0 else pltpu.roll(here, LANES - 1, 1)
                        acc = jnp.where(row_m == m, take(0.5 * (here + other), col_n * 2), acc)
                else:
                    for m in range(HALF):
                        here = read(axis, 2 * m)
                        other = read(axis, 2 * m + 1) if which == 0 else [pltpu.roll(v, LANES - EDGE, 1) for v in here]
                        for h in range(2):
                            got = take(0.5 * (here[h] + other[h]), (col_n % 4) * 32)
                            acc = jnp.where((row_m == m) & (col_n // 4 == h), got, acc)
                kept.append(acc)
            tab_r[d * fine_rows + ROWS * g : d * fine_rows + ROWS * g + ROWS, :] = jnp.where(
                lane < 64, kept[0], kept[1]
            )

    listed.wait()
    slot_of = [pairs[r, 0] for r in range(pair_count)]
    face_of = [pairs[r, 1] for r in range(pair_count)]
    owner_of = [pairs[r, 2] for r in range(pair_count)]
    table_row = [face_of[r] * fine_rows + fine_row(slot_of[r]) for r in range(pair_count)]
    message_row = []
    for r in range(pair_count):
        rank = jnp.int32(0)
        for q in range(r):
            rank = rank + jnp.where(owner_of[q] == owner_of[r], 1, 0)
        message_row.append(owner_of[r] * ROWS + rank)

    box = lax.broadcasted_iota(jnp.int32, (peers * ROWS, LANES), 0)
    message = jnp.full((peers * ROWS, LANES), -1.0, jnp.float32)
    for r in range(pair_count):
        code = pairs[r, 3] * 12 + face_of[r] * 4 + pairs[r, 4] * 2 + pairs[r, 5]
        values = tab_r[pl.ds(table_row[r], 1), :]
        message = jnp.where(box == message_row[r], values, message)
        message = jnp.where(box == message_row[r] + CAP, code.astype(jnp.float32), message)
    send1[...] = message

    pl.semaphore_wait(barrier, peers - 1 + groups - 1)

    def slot(ref, p):
        return ref.at[pl.ds(pl.multiple_of(p * ROWS, ROWS), ROWS)]

    def out1(p):
        return pltpu.make_async_remote_copy(
            src_ref=slot(send1, p), dst_ref=slot(recv1, me), send_sem=s1_sem,
            recv_sem=r1_sem, device_id=(p, mg), device_id_type=MESH,
        )

    def out2(p):
        return pltpu.make_async_remote_copy(
            src_ref=slot(send2, p), dst_ref=slot(recv2, me), send_sem=s2_sem,
            recv_sem=r2_sem, device_id=(p, mg), device_id_type=MESH,
        )

    def outg(g):
        return pltpu.make_async_remote_copy(
            src_ref=gmax, dst_ref=slot(gmax_in, mg), send_sem=sg_sem,
            recv_sem=rg_sem, device_id=(me, g), device_id_type=MESH,
        )

    def drain(ref, sem, count):
        part = ref.at[pl.ds(0, ROWS * count)]
        pltpu.make_async_copy(part, part, sem).wait()

    each_peer(lambda p: out1(p).start())

    loads[2].wait()
    loads[3].wait()
    best = emf_pass([(blocked(cb, g), blocked(cv, g)) for g in range(coarse_groups)], emf_c, best)
    gmax[...] = best
    each_group(lambda g: outg(g).start())

    curl_pass(emf_f, [strided_put(curl_f, s) for s in fine_starts])


    def gathered_rows(read, d, h):
        out = jnp.zeros((ROWS, LANES), jnp.float32)
        for m in range(HALF):
            here = read(d, h * HALF + m)[0]
            out = jnp.where(lane // EDGE == m, here if m == 0 else pltpu.roll(here, EDGE * m, 1), out)
        return out

    def normal_curl(g):
        edge = blocked(emf_c, g)

        def read(d, i):
            after = (i + 1) % EDGE
            if d == 0:
                e_y, e_z = edge(1, i), edge(2, i)
                return sub2(sub2(ahead_y(e_z), e_z), sub2(ahead_z(e_y), e_y))
            if d == 1:
                e_x, e_z = edge(0, i)[:1], edge(2, i)
                return ((ahead_z(e_x)[0] - e_x[0]) - (edge(2, after)[0] - e_z[0]),)
            e_x, e_y = edge(0, i), edge(1, i)
            return sub2(sub2(edge(1, after), e_y), sub2(ahead_y(e_x), e_x))

        return read

    def quadrants(read, g, second):
        def put(d, q1, q2, value):
            n = (g * 12 + d * 4 + q1 * 2 + q2) * ROWS
            if second:
                value = jnp.where(lane < 64, rep[n : n + ROWS, :], value)
            rep[n : n + ROWS, :] = value

        plane = read(0, 0)
        for d in range(2):
            for q1 in range(2):
                face = plane[q1] if d == 0 else gathered_rows(read, 1, q1)
                for q2 in range(2):
                    put(d, q1, q2, take(face, row_m * EDGE + q2 * HALF + col_n))
        for q1 in range(2):
            got = [jnp.zeros((ROWS, LANES), jnp.float32)] * 2
            for m in range(HALF):
                pair = read(2, q1 * HALF + m)
                got = [
                    jnp.where(row_m == m, take(pair[q2], col_n * EDGE), got[q2]) for q2 in range(2)
                ]
            for q2 in range(2):
                put(2, q1, q2, got[q2])

    for g in range(coarse_groups):
        quadrants(blocked(cb, g), g, False)

    slot(recv1, me)[...] = slot(send1, me)[...]
    drain(recv1, r1_sem, peers - 1)
    codes = [
        [((sub + ROWS * g) * 12 + dq).astype(jnp.float32) for dq in range(12)]
        for g in range(coarse_groups)
    ]

    def row_of(ref, n):
        return jnp.broadcast_to(ref[pl.ds(n, 1), :], (ROWS, LANES))

    def collect(p, held):
        for c in range(CAP):
            values, key = row_of(recv1, p * ROWS + c), row_of(recv1, p * ROWS + CAP + c)
            held = [
                [jnp.where(key == codes[g][dq], values, held[g][dq]) for dq in range(12)]
                for g in range(coarse_groups)
            ]
        return held

    empty = jnp.full((ROWS, LANES), EMPTY, jnp.float32)
    held = lax.fori_loop(0, peers, collect, [[empty] * 12 for _ in range(coarse_groups)], unroll=few)
    halves = k_of < HALF
    for g in range(coarse_groups):
        def patch(axis, tile, value, mask):
            where = (axis, slice(ROWS * g, ROWS * g + ROWS), slice(tile * LANES, tile * LANES + LANES))
            put = value < BIG
            if mask is not None:
                put = put & mask
            emf_c[where] = jnp.where(put, value, emf_c[where])

        for d in range(3):
            for which in range(2):
                axis = TANGENT[d][which]
                for q1 in range(2):
                    low, high = held[g][d * 4 + q1 * 2], held[g][d * 4 + q1 * 2 + 1]
                    if d < 2:
                        spread = (lane // EDGE) * HALF + lane % HALF + 64 * which
                        both = jnp.where(halves, take(low, spread), take(high, spread))
                        if d == 0:
                            patch(axis, q1, both, None)
                        else:
                            for m in range(HALF):
                                turned = both if m == 0 else pltpu.roll(both, LANES - EDGE * m, 1)
                                patch(axis, 2 * (q1 * HALF + m), turned, first_y)
                    else:
                        for m in range(HALF):
                            for q2 in range(2):
                                got = take((low, high)[q2], m * HALF + lane // EDGE + 64 * which)
                                patch(axis, 2 * (q1 * HALF + m) + q2, got, first_z)

    for g in range(coarse_groups):
        quadrants(normal_curl(g), g, True)

    drain(gmax_in, rg_sem, groups - 1)
    for k in range(1, groups):
        best = jnp.maximum(best, slot(gmax_in, lax.rem(mg + k, groups))[...])
    top_row = jnp.max(best, axis=0, keepdims=True)

    def answer(p, carry):
        rows = jnp.broadcast_to(top_row, (ROWS, LANES))
        for c in range(CAP):
            key = row_of(recv1, p * ROWS + CAP + c)
            acc = jnp.zeros((ROWS, LANES), jnp.float32)
            for g in range(coarse_groups):
                for dq in range(12):
                    acc = jnp.where(
                        key == codes[g][dq],
                        rep[(g * 12 + dq) * ROWS : (g * 12 + dq + 1) * ROWS, :],
                        acc,
                    )
            rows = jnp.where(sub == c, jnp.sum(acc, axis=0, keepdims=True), rows)
        slot(send2, p)[...] = rows
        return carry

    lax.fori_loop(0, peers, answer, 0, unroll=few)
    each_peer(lambda p: out2(p).start())
    curl_pass(emf_c, [blocked_put(curl_c, g) for g in range(coarse_groups)])

    for g in range(fine_groups):
        for n, read in enumerate((strided(fb, fine_starts[g]), strided(curl_f, fine_starts[g]))):
            for d in range(3):
                for h in range(2):
                    if d == 0:
                        face = read(0, 0)[h]
                    elif d == 1:
                        face = gathered_rows(read, 1, h)
                    else:
                        face = jnp.zeros((ROWS, LANES), jnp.float32)
                        for m in range(HALF):
                            pair = read(2, h * HALF + m)
                            for part in range(2):
                                face = jnp.where(
                                    (lane // EDGE == m) & (k_of // HALF == part),
                                    take(pair[part], (lane % HALF) * EDGE),
                                    face,
                                )
                    tab_n[
                        d * fine_rows + ROWS * g : d * fine_rows + ROWS * g + ROWS,
                        (2 * n + h) * LANES : (2 * n + h + 1) * LANES,
                    ] = face
    for r in range(pair_count):
        picked[r : r + 1, :] = tab_n[pl.ds(table_row[r], 1), :]

    slot(recv2, me)[...] = slot(send2, me)[...]
    drain(recv2, r2_sem, peers - 1)
    top = jnp.full((ROWS, LANES), 0.0, jnp.float32)
    top = lax.fori_loop(0, peers, lambda p, t: jnp.maximum(t, row_of(recv2, p * ROWS + CAP)), top, unroll=few)
    dt = 0.2 / jnp.max(top, axis=1, keepdims=True)
    for r in range(pair_count):
        own[r : r + 1, :] = recv2[pl.ds(message_row[r], 1), :]
    for s in range(0, pair_count, ROWS):
        take_rows = min(ROWS, pair_count - s)
        quad = own[s : s + ROWS, :]
        quad = quad - dt * pltpu.roll(quad, 64, 1)
        for h in range(2):
            coarse = take(quad, (4 * h + lane // 32) * HALF + k_of // 2)
            fine = picked[s : s + ROWS, h * LANES : (h + 1) * LANES] - (dt / 0.5) * picked[
                s : s + ROWS, (2 + h) * LANES : (3 + h) * LANES
            ]
            jump_out[s : s + take_rows, h * LANES : (h + 1) * LANES] = (fine - coarse)[:take_rows]

    def finish(i, carry):
        for g in range(coarse_groups):
            read, put, curl = blocked(cb, g), blocked_put(curl_c, g), blocked(curl_c, g)
            for c in range(3):
                put(c, i, sub2(read(c, i), (dt * curl(c, i)[0], dt * curl(c, i)[1])))
        return carry

    lax.fori_loop(0, EDGE, finish, 0, unroll=2)
    doubled = dt / 0.5
    span = fine_count * 3 * ROWS

    def finish_fine(n, carry):
        part = pl.ds(pl.multiple_of(n * span, ROWS), span)
        curl_f[part, :] = fb[part, :] - doubled[:1] * curl_f[part, :]
        return carry

    lax.fori_loop(0, TILES // ROWS, finish_fine, 0)
    drain(send1, s1_sem, peers - 1)
    drain(send2, s2_sem, peers - 1)
    drain(gmax_in, sg_sem, groups - 1)


def store(curl_c, curl_f, jump, out_c, out_f, out_j, sems):
    copies = [
        pltpu.make_async_copy(src, dst, sems.at[n])
        for n, (src, dst) in enumerate(((curl_c, out_c), (curl_f, out_f), (jump, out_j)))
    ]
    for copy in copies:
        copy.start()
    for copy in copies:
        copy.wait()


def on_device(peers, groups, coarse_field, coarse_velocity, fine_field, fine_velocity, pairs):
    coarse_count, fine_count = coarse_field.shape[1], fine_field.shape[1]
    pair_count = pairs.shape[1]
    cells = EDGE**3
    flat_rows = fine_count * 3 * TILES

    def coarse_view(x):
        return jnp.transpose(x[0], (1, 0, 2))

    def fine_view(x):
        return x.reshape(flat_rows, LANES)

    fine_rows = ROWS * -(-fine_count // ROWS)
    pair_rows = ROWS * -(-pair_count // ROWS)
    cb, cv = coarse_view(coarse_field), coarse_view(coarse_velocity)
    fb, fv = fine_view(fine_field), fine_view(fine_velocity)
    operands = [
        pltpu.with_memory_space_constraint(x, pltpu.HBM) for x in (pairs[0], cb, cv, fb, fv)
    ]
    f32 = jnp.float32
    dma = pltpu.SemaphoreType.DMA
    vmem = pltpu.VMEM
    anywhere = pl.BlockSpec(memory_space=pltpu.HBM)
    inside = pl.BlockSpec(memory_space=pltpu.VMEM)
    coarse_shape, fine_shape = (3, coarse_count, cells), (flat_rows, LANES)
    new_c, new_f, jump = pl.pallas_call(
        functools.partial(kernel, peers, groups, coarse_count, fine_count, pair_count),
        out_shape=(
            jax.ShapeDtypeStruct(coarse_shape, f32),
            jax.ShapeDtypeStruct(fine_shape, f32),
            jax.ShapeDtypeStruct((pair_count, EDGE * EDGE), f32),
        ),
        in_specs=[anywhere] * 5,
        out_specs=(inside,) * 3,
        scratch_shapes=[
            pltpu.SMEM(pairs.shape[1:], jnp.int32),
            vmem(coarse_shape, f32),
            vmem(coarse_shape, f32),
            vmem(fine_shape, f32),
            vmem(fine_shape, f32),
            vmem(coarse_shape, f32),
            vmem((3, fine_rows, cells), f32),
            vmem((3 * fine_rows, LANES), f32),
            vmem((3 * fine_rows, 4 * LANES), f32),
            vmem((12 * coarse_count, LANES), f32),
            vmem((pair_rows, LANES), f32),
            vmem((pair_rows, 4 * LANES), f32),
            vmem((peers * ROWS, LANES), f32),
            vmem((peers * ROWS, LANES), f32),
            vmem((peers * ROWS, LANES), f32),
            vmem((peers * ROWS, LANES), f32),
            vmem((ROWS, LANES), f32),
            vmem((groups * ROWS, LANES), f32),
            dma((5,)),
            dma,
            dma,
            dma,
            dma,
            dma,
            dma,
        ],
        compiler_params=pltpu.CompilerParams(
            collective_id=0, has_side_effects=True, vmem_limit_bytes=32 * 1024 * 1024
        ),
    )(*operands)
    coarse_out, fine_out, jump = pl.pallas_call(
        store,
        out_shape=(
            jax.ShapeDtypeStruct(coarse_shape, f32),
            jax.ShapeDtypeStruct(fine_shape, f32),
            jax.ShapeDtypeStruct((pair_count, EDGE * EDGE), f32),
        ),
        in_specs=[inside] * 3,
        out_specs=(anywhere,) * 3,
        scratch_shapes=[dma((3,))],
    )(*(pltpu.with_memory_space_constraint(x, pltpu.VMEM) for x in (new_c, new_f, jump)))
    return (
        jnp.transpose(coarse_out, (1, 0, 2))[None],
        fine_out.reshape(1, fine_count, 3, cells),
        jump[None],
    )


def solution(mesh):
    spec = P("gz", "blocks", None, None)
    flat = P("gz", "blocks", None)
    return jax.shard_map(
        functools.partial(on_device, mesh.shape["blocks"], mesh.shape["gz"]),
        mesh=mesh,
        in_specs=(spec, spec, spec, spec, flat),
        out_specs=(spec, spec, flat),
        check_vma=False,
    )
```

```python
import functools

import jax
import jax.numpy as jnp
from jax import lax
from jax.experimental import pallas as pl
from jax.experimental.pallas import tpu as pltpu
from jax.sharding import PartitionSpec as P

EDGE = 16
HALF = 8
CAP = 2
LANES = 128
ROWS = 8
TILES = EDGE**3 // LANES
BIG = 1e30
EMPTY = 3e38
TANGENT = ((1, 2), (0, 2), (0, 1))
MESH = pl.DeviceIdType.MESH


def take(values, index):
    return jnp.take_along_axis(values, index, axis=1, mode="promise_in_bounds")


def kernel(
    peers,
    groups,
    coarse_count,
    fine_count,
    pair_count,
    pairs_hbm,
    cb_hbm,
    cv_hbm,
    fb_hbm,
    fv_hbm,
    curl_c,
    curl_f,
    jump_out,
    pairs,
    cb,
    cv,
    fb,
    fv,
    emf_c,
    emf_f,
    tab_r,
    tab_n,
    rep,
    own,
    picked,
    send1,
    recv1,
    send2,
    recv2,
    gmax,
    gmax_in,
    load_sem,
    s1_sem,
    r1_sem,
    s2_sem,
    r2_sem,
    sg_sem,
    rg_sem,
):
    me = lax.axis_index("blocks")
    mg = lax.axis_index("gz")
    few = peers <= 8

    def each_peer(body):
        lax.fori_loop(1, peers, lambda k, _: (body(lax.rem(me + k, peers)), 0)[1], 0, unroll=few)

    def each_group(body):
        for k in range(1, groups):
            body(lax.rem(mg + k, groups))

    coarse_groups = coarse_count // ROWS
    fine_groups = -(-fine_count // ROWS)
    fine_starts = [min(ROWS * g, fine_count - ROWS) for g in range(fine_groups)]
    fine_rows = ROWS * fine_groups
    arrivals = ((fb_hbm, fb), (fv_hbm, fv), (cb_hbm, cb), (cv_hbm, cv))
    listed = pltpu.make_async_copy(pairs_hbm, pairs, load_sem.at[4])
    listed.start()
    for n, (src, dst) in enumerate(arrivals):
        if n >= 2:
            pltpu.make_async_copy(src, dst, load_sem.at[n]).start()
        else:
            for c in range(3):
                for g, start in enumerate(fine_starts):
                    pltpu.make_async_copy(
                        src.at[pl.ds(start, ROWS), c, 0],
                        dst.at[c, pl.ds(ROWS * g, ROWS)],
                        load_sem.at[n],
                    ).start()

    def loaded(n):
        pltpu.make_async_copy(arrivals[n][1], arrivals[n][1], load_sem.at[n]).wait()

    barrier = pltpu.get_barrier_semaphore()
    each_peer(
        lambda p: pl.semaphore_signal(barrier, inc=1, device_id=(p, mg), device_id_type=MESH)
    )
    each_group(
        lambda g: pl.semaphore_signal(barrier, inc=1, device_id=(me, g), device_id_type=MESH)
    )

    lane = lax.broadcasted_iota(jnp.int32, (ROWS, LANES), 1)
    sub = lax.broadcasted_iota(jnp.int32, (ROWS, LANES), 0)
    k_of = lane % EDGE
    first_y = lane < EDGE
    last_y = lane >= LANES - EDGE
    first_z = k_of == 0
    last_z = k_of == EDGE - 1

    def back_y(pair):
        low, high = pltpu.roll(pair[0], EDGE, 1), pltpu.roll(pair[1], EDGE, 1)
        return jnp.where(first_y, high, low), jnp.where(first_y, low, high)

    def ahead_y(pair):
        low, high = pltpu.roll(pair[0], LANES - EDGE, 1), pltpu.roll(pair[1], LANES - EDGE, 1)
        return jnp.where(last_y, high, low), jnp.where(last_y, low, high)

    def back_z(pair):
        return tuple(
            jnp.where(first_z, pltpu.roll(v, LANES - EDGE + 1, 1), pltpu.roll(v, 1, 1))
            for v in pair
        )

    def ahead_z(pair):
        return tuple(
            jnp.where(last_z, pltpu.roll(v, EDGE - 1, 1), pltpu.roll(v, LANES - 1, 1))
            for v in pair
        )

    def add(a, b):
        return a[0] + b[0], a[1] + b[1]

    def sub2(a, b):
        return a[0] - b[0], a[1] - b[1]

    def mul(a, b):
        return a[0] * b[0], a[1] * b[1]

    def scale(s, a):
        return s * a[0], s * a[1]

    def column(tile):
        return pl.ds(pl.multiple_of(tile * LANES, LANES), LANES)

    def blocked(ref, g):
        def read(c, i):
            return tuple(ref[c, ROWS * g : ROWS * g + ROWS, column(2 * i + h)] for h in range(2))

        return read

    def blocked_put(ref, g):
        def put(c, i, pair):
            for h in range(2):
                ref[c, ROWS * g : ROWS * g + ROWS, column(2 * i + h)] = pair[h]

        return put

    def cells(field, velocity, i, want_speed):
        after = lax.rem(i + 1, EDGE)
        b_x, b_y, b_z = field(0, i), field(1, i), field(2, i)
        c_x = scale(0.5, add(b_x, field(0, after)))
        c_y = scale(0.5, add(b_y, ahead_y(b_y)))
        c_z = scale(0.5, add(b_z, ahead_z(b_z)))
        v_x, v_y, v_z = velocity(0, i), velocity(1, i), velocity(2, i)
        cell_y = sub2(mul(v_x, c_z), mul(v_z, c_x))
        cell_z = sub2(mul(v_y, c_x), mul(v_x, c_y))
        part_y = scale(0.25, add(cell_y, back_z(cell_y)))
        part_z = scale(0.25, add(cell_z, back_y(cell_z)))
        if not want_speed:
            return part_y, part_z
        cell_x = sub2(mul(v_z, c_y), mul(v_y, c_z))
        part_x = scale(0.25, add(cell_x, back_y(cell_x)))
        e_x = add(part_x, back_z(part_x))
        vv = add(add(mul(v_x, v_x), mul(v_y, v_y)), mul(v_z, v_z))
        cc = add(add(mul(c_x, c_x), mul(c_y, c_y)), mul(c_z, c_z))
        speed = jnp.maximum(
            jnp.sqrt(vv[0]) + jnp.sqrt(cc[0]), jnp.sqrt(vv[1]) + jnp.sqrt(cc[1])
        )
        return part_y, part_z, e_x, speed

    def emf_pass(sources, target, best):
        starts = [cells(f, v, EDGE - 1, False) for f, v in sources]

        def step(i, carry):
            parts, top = carry
            fresh = []
            for g, (f, v) in enumerate(sources):
                part_y, part_z, e_x, speed = cells(f, v, i, True)
                put = blocked_put(target, g)
                put(0, i, e_x)
                put(1, i, add(part_y, parts[g][0]))
                put(2, i, add(part_z, parts[g][1]))
                top = jnp.maximum(top, speed)
                fresh.append((part_y, part_z))
            return fresh, top

        return lax.fori_loop(0, EDGE, step, (starts, best))[1]

    def curl_pass(emf, puts):
        def step(i, carry):
            after = lax.rem(i + 1, EDGE)
            for g, put in enumerate(puts):
                read = blocked(emf, g)
                e_x, e_y, e_z = read(0, i), read(1, i), read(2, i)
                put(0, i, sub2(sub2(ahead_y(e_z), e_z), sub2(ahead_z(e_y), e_y)))
                put(1, i, sub2(sub2(ahead_z(e_x), e_x), sub2(read(2, after), e_z)))
                put(2, i, sub2(sub2(read(1, after), e_y), sub2(ahead_y(e_x), e_x)))
            return carry

        lax.fori_loop(0, EDGE, step, 0)


    def fine_row(slot):
        last = ROWS * (fine_groups - 1)
        return jnp.where(slot < last, slot, slot - fine_starts[-1] + last)

    loaded(0)
    loaded(1)
    best = emf_pass([(blocked(fb, g), blocked(fv, g)) for g in range(fine_groups)], emf_f, jnp.zeros((ROWS, LANES), jnp.float32))

    within = lane % 64
    row_m, col_n = within // HALF, within % HALF
    face_x = (row_m % 4) * 32 + col_n * 2
    for g in range(fine_groups):
        read = blocked(emf_f, g)
        for d in range(3):
            kept = []
            for which in range(2):
                axis = TANGENT[d][which]
                acc = jnp.zeros((ROWS, LANES), jnp.float32)
                if d == 0:
                    pair = read(axis, 0)
                    shift = EDGE if which == 0 else 1
                    for h in range(2):
                        mean = 0.5 * (pair[h] + pltpu.roll(pair[h], LANES - shift, 1))
                        acc = jnp.where(row_m // 4 == h, take(mean, face_x), acc)
                elif d == 1:
                    for m in range(HALF):
                        here = read(axis, 2 * m)[0]
                        other = read(axis, 2 * m + 1)[0] if which == 0 else pltpu.roll(here, LANES - 1, 1)
                        acc = jnp.where(row_m == m, take(0.5 * (here + other), col_n * 2), acc)
                else:
                    for m in range(HALF):
                        here = read(axis, 2 * m)
                        other = read(axis, 2 * m + 1) if which == 0 else [pltpu.roll(v, LANES - EDGE, 1) for v in here]
                        for h in range(2):
                            got = take(0.5 * (here[h] + other[h]), (col_n % 4) * 32)
                            acc = jnp.where((row_m == m) & (col_n // 4 == h), got, acc)
                kept.append(acc)
            tab_r[d * fine_rows + ROWS * g : d * fine_rows + ROWS * g + ROWS, :] = jnp.where(
                lane < 64, kept[0], kept[1]
            )

    listed.wait()
    slot_of = [pairs[r, 0] for r in range(pair_count)]
    face_of = [pairs[r, 1] for r in range(pair_count)]
    owner_of = [pairs[r, 2] for r in range(pair_count)]
    table_row = [face_of[r] * fine_rows + fine_row(slot_of[r]) for r in range(pair_count)]
    message_row = []
    for r in range(pair_count):
        rank = jnp.int32(0)
        for q in range(r):
            rank = rank + jnp.where(owner_of[q] == owner_of[r], 1, 0)
        message_row.append(owner_of[r] * ROWS + rank)

    box = lax.broadcasted_iota(jnp.int32, (peers * ROWS, LANES), 0)
    message = jnp.full((peers * ROWS, LANES), -1.0, jnp.float32)
    for r in range(pair_count):
        code = pairs[r, 3] * 12 + face_of[r] * 4 + pairs[r, 4] * 2 + pairs[r, 5]
        values = tab_r[pl.ds(table_row[r], 1), :]
        message = jnp.where(box == message_row[r], values, message)
        message = jnp.where(box == message_row[r] + CAP, code.astype(jnp.float32), message)
    send1[...] = message

    pl.semaphore_wait(barrier, peers - 1 + groups - 1)

    def slot(ref, p):
        return ref.at[pl.ds(pl.multiple_of(p * ROWS, ROWS), ROWS)]

    def out1(p):
        return pltpu.make_async_remote_copy(
            src_ref=slot(send1, p), dst_ref=slot(recv1, me), send_sem=s1_sem,
            recv_sem=r1_sem, device_id=(p, mg), device_id_type=MESH,
        )

    def out2(p):
        return pltpu.make_async_remote_copy(
            src_ref=slot(send2, p), dst_ref=slot(recv2, me), send_sem=s2_sem,
            recv_sem=r2_sem, device_id=(p, mg), device_id_type=MESH,
        )

    def outg(g):
        return pltpu.make_async_remote_copy(
            src_ref=gmax, dst_ref=slot(gmax_in, mg), send_sem=sg_sem,
            recv_sem=rg_sem, device_id=(me, g), device_id_type=MESH,
        )

    def drain(ref, sem, count):
        part = ref.at[pl.ds(0, ROWS * count)]
        pltpu.make_async_copy(part, part, sem).wait()

    each_peer(lambda p: out1(p).start())

    loaded(2)
    loaded(3)
    best = emf_pass([(blocked(cb, g), blocked(cv, g)) for g in range(coarse_groups)], emf_c, best)
    gmax[...] = best
    each_group(lambda g: outg(g).start())

    curl_pass(emf_f, [blocked_put(curl_f, g) for g in range(fine_groups)])


    def gathered_rows(read, d, h):
        out = jnp.zeros((ROWS, LANES), jnp.float32)
        for m in range(HALF):
            here = read(d, h * HALF + m)[0]
            out = jnp.where(lane // EDGE == m, here if m == 0 else pltpu.roll(here, EDGE * m, 1), out)
        return out

    def normal_curl(g):
        edge = blocked(emf_c, g)

        def read(d, i):
            after = (i + 1) % EDGE
            if d == 0:
                e_y, e_z = edge(1, i), edge(2, i)
                return sub2(sub2(ahead_y(e_z), e_z), sub2(ahead_z(e_y), e_y))
            if d == 1:
                e_x, e_z = edge(0, i)[:1], edge(2, i)
                return ((ahead_z(e_x)[0] - e_x[0]) - (edge(2, after)[0] - e_z[0]),)
            e_x, e_y = edge(0, i), edge(1, i)
            return sub2(sub2(edge(1, after), e_y), sub2(ahead_y(e_x), e_x))

        return read

    def quadrants(read, g, second):
        def put(d, q1, q2, value):
            n = (g * 12 + d * 4 + q1 * 2 + q2) * ROWS
            if second:
                value = jnp.where(lane < 64, rep[n : n + ROWS, :], value)
            rep[n : n + ROWS, :] = value

        plane = read(0, 0)
        for d in range(2):
            for q1 in range(2):
                face = plane[q1] if d == 0 else gathered_rows(read, 1, q1)
                for q2 in range(2):
                    put(d, q1, q2, take(face, row_m * EDGE + q2 * HALF + col_n))
        for q1 in range(2):
            got = [jnp.zeros((ROWS, LANES), jnp.float32)] * 2
            for m in range(HALF):
                pair = read(2, q1 * HALF + m)
                got = [
                    jnp.where(row_m == m, take(pair[q2], col_n * EDGE), got[q2]) for q2 in range(2)
                ]
            for q2 in range(2):
                put(2, q1, q2, got[q2])

    for g in range(coarse_groups):
        quadrants(blocked(cb, g), g, False)

    slot(recv1, me)[...] = slot(send1, me)[...]
    drain(recv1, r1_sem, peers - 1)
    codes = [
        [((sub + ROWS * g) * 12 + dq).astype(jnp.float32) for dq in range(12)]
        for g in range(coarse_groups)
    ]

    def row_of(ref, n):
        return jnp.broadcast_to(ref[pl.ds(n, 1), :], (ROWS, LANES))

    def collect(p, held):
        for c in range(CAP):
            values, key = row_of(recv1, p * ROWS + c), row_of(recv1, p * ROWS + CAP + c)
            held = [
                [jnp.where(key == codes[g][dq], values, held[g][dq]) for dq in range(12)]
                for g in range(coarse_groups)
            ]
        return held

    empty = jnp.full((ROWS, LANES), EMPTY, jnp.float32)
    held = lax.fori_loop(0, peers, collect, [[empty] * 12 for _ in range(coarse_groups)], unroll=few)
    halves = k_of < HALF
    for g in range(coarse_groups):
        def patch(axis, tile, value, mask):
            where = (axis, slice(ROWS * g, ROWS * g + ROWS), slice(tile * LANES, tile * LANES + LANES))
            put = value < BIG
            if mask is not None:
                put = put & mask
            emf_c[where] = jnp.where(put, value, emf_c[where])

        for d in range(3):
            for which in range(2):
                axis = TANGENT[d][which]
                for q1 in range(2):
                    low, high = held[g][d * 4 + q1 * 2], held[g][d * 4 + q1 * 2 + 1]
                    if d < 2:
                        spread = (lane // EDGE) * HALF + lane % HALF + 64 * which
                        both = jnp.where(halves, take(low, spread), take(high, spread))
                        if d == 0:
                            patch(axis, q1, both, None)
                        else:
                            for m in range(HALF):
                                turned = both if m == 0 else pltpu.roll(both, LANES - EDGE * m, 1)
                                patch(axis, 2 * (q1 * HALF + m), turned, first_y)
                    else:
                        for m in range(HALF):
                            for q2 in range(2):
                                got = take((low, high)[q2], m * HALF + lane // EDGE + 64 * which)
                                patch(axis, 2 * (q1 * HALF + m) + q2, got, first_z)

    for g in range(coarse_groups):
        quadrants(normal_curl(g), g, True)

    drain(gmax_in, rg_sem, groups - 1)
    for k in range(1, groups):
        best = jnp.maximum(best, slot(gmax_in, lax.rem(mg + k, groups))[...])
    top_row = jnp.max(best, axis=0, keepdims=True)

    def answer(p, carry):
        rows = jnp.broadcast_to(top_row, (ROWS, LANES))
        for c in range(CAP):
            key = row_of(recv1, p * ROWS + CAP + c)
            acc = jnp.zeros((ROWS, LANES), jnp.float32)
            for g in range(coarse_groups):
                for dq in range(12):
                    acc = jnp.where(
                        key == codes[g][dq],
                        rep[(g * 12 + dq) * ROWS : (g * 12 + dq + 1) * ROWS, :],
                        acc,
                    )
            rows = jnp.where(sub == c, jnp.sum(acc, axis=0, keepdims=True), rows)
        slot(send2, p)[...] = rows
        return carry

    lax.fori_loop(0, peers, answer, 0, unroll=few)
    each_peer(lambda p: out2(p).start())
    curl_pass(emf_c, [blocked_put(curl_c, g) for g in range(coarse_groups)])

    for g in range(fine_groups):
        for n, read in enumerate((blocked(fb, g), blocked(curl_f, g))):
            for d in range(3):
                for h in range(2):
                    if d == 0:
                        face = read(0, 0)[h]
                    elif d == 1:
                        face = gathered_rows(read, 1, h)
                    else:
                        face = jnp.zeros((ROWS, LANES), jnp.float32)
                        for m in range(HALF):
                            pair = read(2, h * HALF + m)
                            for part in range(2):
                                face = jnp.where(
                                    (lane // EDGE == m) & (k_of // HALF == part),
                                    take(pair[part], (lane % HALF) * EDGE),
                                    face,
                                )
                    tab_n[
                        d * fine_rows + ROWS * g : d * fine_rows + ROWS * g + ROWS,
                        (2 * n + h) * LANES : (2 * n + h + 1) * LANES,
                    ] = face
    for r in range(pair_count):
        picked[r : r + 1, :] = tab_n[pl.ds(table_row[r], 1), :]

    slot(recv2, me)[...] = slot(send2, me)[...]
    drain(recv2, r2_sem, peers - 1)
    top = jnp.full((ROWS, LANES), 0.0, jnp.float32)
    top = lax.fori_loop(0, peers, lambda p, t: jnp.maximum(t, row_of(recv2, p * ROWS + CAP)), top, unroll=few)
    dt = 0.2 / jnp.max(top, axis=1, keepdims=True)
    for r in range(pair_count):
        own[r : r + 1, :] = recv2[pl.ds(message_row[r], 1), :]
    for s in range(0, pair_count, ROWS):
        take_rows = min(ROWS, pair_count - s)
        quad = own[s : s + ROWS, :]
        quad = quad - dt * pltpu.roll(quad, 64, 1)
        for h in range(2):
            coarse = take(quad, (4 * h + lane // 32) * HALF + k_of // 2)
            fine = picked[s : s + ROWS, h * LANES : (h + 1) * LANES] - (dt / 0.5) * picked[
                s : s + ROWS, (2 + h) * LANES : (3 + h) * LANES
            ]
            jump_out[s : s + take_rows, h * LANES : (h + 1) * LANES] = (fine - coarse)[:take_rows]

    def finish(i, carry):
        for field, update, factor, count in (
            (cb, curl_c, dt, coarse_groups),
            (fb, curl_f, dt / 0.5, fine_groups),
        ):
            for g in range(count):
                read, put, curl = blocked(field, g), blocked_put(update, g), blocked(update, g)
                for c in range(3):
                    low, high = curl(c, i)
                    put(c, i, sub2(read(c, i), (factor * low, factor * high)))
        return carry

    lax.fori_loop(0, EDGE, finish, 0, unroll=2)
    drain(send1, s1_sem, peers - 1)
    drain(send2, s2_sem, peers - 1)
    drain(gmax_in, sg_sem, groups - 1)


def store(new_c, new_f, jump, out_c, out_f, out_j, sems):
    count = out_f.shape[0]
    fine_groups = new_f.shape[1] // ROWS

    def fine(g, c):
        start = min(ROWS * g, count - ROWS)
        return pltpu.make_async_copy(
            new_f.at[c, pl.ds(ROWS * g, ROWS)],
            out_f.at[pl.ds(start, ROWS), c, 0],
            sems.at[2 + 3 * g + c],
        )

    last = [fine(fine_groups - 1, c) for c in range(3)]
    rest = [
        pltpu.make_async_copy(new_c, out_c, sems.at[0]),
        pltpu.make_async_copy(jump, out_j, sems.at[1]),
    ]
    for copy in last + rest:
        copy.start()
    for copy in last:
        copy.wait()
    before = [fine(g, c) for g in range(fine_groups - 1) for c in range(3)]
    for copy in before:
        copy.start()
    for copy in rest + before:
        copy.wait()


def on_device(peers, groups, coarse_field, coarse_velocity, fine_field, fine_velocity, pairs):
    coarse_count, fine_count = coarse_field.shape[1], fine_field.shape[1]
    pair_count = pairs.shape[1]
    cells = EDGE**3

    def coarse_view(x):
        return jnp.transpose(x[0], (1, 0, 2))

    def fine_view(x):
        return jnp.transpose(x, (1, 2, 0, 3))

    fine_rows = ROWS * -(-fine_count // ROWS)
    pair_rows = ROWS * -(-pair_count // ROWS)
    cb, cv = coarse_view(coarse_field), coarse_view(coarse_velocity)
    fb, fv = fine_view(fine_field), fine_view(fine_velocity)
    operands = [
        pltpu.with_memory_space_constraint(x, pltpu.HBM) for x in (pairs[0], cb, cv, fb, fv)
    ]
    f32 = jnp.float32
    dma = pltpu.SemaphoreType.DMA
    vmem = pltpu.VMEM
    anywhere = pl.BlockSpec(memory_space=pltpu.HBM)
    inside = pl.BlockSpec(memory_space=pltpu.VMEM)
    coarse_shape, fine_shape = (3, coarse_count, cells), (3, fine_rows, cells)
    new_c, new_f, jump = pl.pallas_call(
        functools.partial(kernel, peers, groups, coarse_count, fine_count, pair_count),
        out_shape=(
            jax.ShapeDtypeStruct(coarse_shape, f32),
            jax.ShapeDtypeStruct(fine_shape, f32),
            jax.ShapeDtypeStruct((pair_count, EDGE * EDGE), f32),
        ),
        in_specs=[anywhere] * 5,
        out_specs=(inside,) * 3,
        scratch_shapes=[
            pltpu.SMEM(pairs.shape[1:], jnp.int32),
            vmem(coarse_shape, f32),
            vmem(coarse_shape, f32),
            vmem(fine_shape, f32),
            vmem(fine_shape, f32),
            vmem(coarse_shape, f32),
            vmem((3, fine_rows, cells), f32),
            vmem((3 * fine_rows, LANES), f32),
            vmem((3 * fine_rows, 4 * LANES), f32),
            vmem((12 * coarse_count, LANES), f32),
            vmem((pair_rows, LANES), f32),
            vmem((pair_rows, 4 * LANES), f32),
            vmem((peers * ROWS, LANES), f32),
            vmem((peers * ROWS, LANES), f32),
            vmem((peers * ROWS, LANES), f32),
            vmem((peers * ROWS, LANES), f32),
            vmem((ROWS, LANES), f32),
            vmem((groups * ROWS, LANES), f32),
            dma((5,)),
            dma,
            dma,
            dma,
            dma,
            dma,
            dma,
        ],
        compiler_params=pltpu.CompilerParams(
            collective_id=0, has_side_effects=True, vmem_limit_bytes=32 * 1024 * 1024
        ),
    )(*operands)
    coarse_out, fine_out, jump = pl.pallas_call(
        store,
        out_shape=(
            jax.ShapeDtypeStruct(coarse_shape, f32),
            jax.ShapeDtypeStruct((fine_count, 3, 1, cells), f32),
            jax.ShapeDtypeStruct((pair_count, EDGE * EDGE), f32),
        ),
        in_specs=[inside] * 3,
        out_specs=(anywhere,) * 3,
        scratch_shapes=[dma((2 + 3 * (fine_rows // ROWS),))],
    )(*(pltpu.with_memory_space_constraint(x, pltpu.VMEM) for x in (new_c, new_f, jump)))
    return (
        jnp.transpose(coarse_out, (1, 0, 2))[None],
        jnp.transpose(fine_out, (2, 0, 1, 3)),
        jump[None],
    )


def solution(mesh):
    spec = P("gz", "blocks", None, None)
    flat = P("gz", "blocks", None)
    return jax.shard_map(
        functools.partial(on_device, mesh.shape["blocks"], mesh.shape["gz"]),
        mesh=mesh,
        in_specs=(spec, spec, spec, spec, flat),
        out_specs=(spec, spec, flat),
        check_vma=False,
    )
```
